256 devices in a mesh: seq: 64 (over x, z_lo, y, core), tensor: 4 (over z_hi).
Axes of the slice: x: 4, y: 4, z: 8 (z_hi: 4, z_lo: 2; z = z_hi * 2 + z_lo), core: 2. Of those that a mesh axis runs over, the one named last changes fastest.
Arguments:
- q_tok: bfloat16 [32768, 1536], P('seq', 'tensor'), may hold values from -24 to 24
- k_tok: bfloat16 [32768, 1536], P('seq', 'tensor'), may hold values from -6 to 6
- v_tok: bfloat16 [32768, 1536], P('seq', 'tensor'), may hold values from -16 to 16
- ref_hidden: bfloat16 [2048, 3072], P('seq', 'tensor'), may hold values from -16 to 16
- ref_wk: bfloat16 [3072, 1536], P('tensor'), may hold values from -0.109375 to 0.109375
- ref_wv: bfloat16 [3072, 1536], P('tensor'), may hold values from -0.109375 to 0.109375
- key_gain: float32 [128], replicated, may hold values from 1 to 2
Outputs:
- attended: bfloat16 [32768, 1536], P('seq', 'tensor')
The draws below stay inside these ranges and needn't reach their ends.
All inputs are finite; a program needn't handle non-finite values.
Results may differ from the reference program's by a relative error of at most 0.022.
Values may be sent and summed in bfloat16 or wider, within the bound.
No kernel may reach another device: no remote copies, remote signals or barrier semaphores. Data moves between devices by JAX's collectives and lax.ppermute only.
A program may use at most 128 MiB of HBM per device.

```python
import jax
import jax.numpy as jnp
from jax import lax

D = 3072
HEADS = 12
HD = 128
VIEW_LEN = 4096
TOKENS = 32768
REF_LEN = 2048


def draw_pair(key):
    base = jax.random.fold_in(key, 11)
    key_query, key_keys = jax.random.split(base, 2)
    shape = (TOKENS, HEADS * HD)
    queries = jnp.clip(1.5 * jax.random.normal(key_query, shape, jnp.float32), -6.0, 6.0)
    key_rows = jnp.clip(1.5 * jax.random.normal(key_keys, shape, jnp.float32), -6.0, 6.0)
    return (jnp.clip(queries, -24.0, 24.0), key_rows)


def draw_q_tok(key, part):
    return draw_pair(key)[0].astype(jnp.bfloat16)


def draw_k_tok(key, part):
    return draw_pair(key)[1].astype(jnp.bfloat16)


def steps_of(stream_key, extent, pieces, low, top_value):
    gain, own = 1.0, jax.random.fold_in(stream_key, 6)
    for position, shards_of in pieces:
        steps = jnp.exp(jax.random.uniform(jax.random.fold_in(own, position), (shards_of,), jnp.float32, low / len(pieces), top_value / len(pieces)))
        gain = gain * jnp.repeat(steps, extent[position] // shards_of).reshape([-1 if axis == position else 1 for axis in range(len(extent))])
    return gain


def scatter_about(key, dims, spread, limit, cuts=(), kind=jnp.bfloat16):
    result = spread * jax.random.normal(key, dims, jnp.float32)
    if cuts:
        result = result * steps_of(key, dims, cuts, -0.22, 0.18)
    return jnp.clip(result, -limit, limit).astype(kind)


def setup_inputs(seed: int = 0) -> dict:
    keys = jax.random.split(jax.random.key(seed), 8)
    q_tok = draw_q_tok(jax.random.fold_in(keys[7], 71), 0)
    k_tok = draw_k_tok(jax.random.fold_in(keys[7], 71), 0)
    v_tok = scatter_about(keys[2], (TOKENS, HEADS * HD), 3.0, 16.0, ((0, 64), (1, 4)))
    ref_hidden = scatter_about(keys[3], (REF_LEN, D), 3.0, 16.0, ((0, 64), (1, 4)))
    ref_wk = scatter_about(keys[4], (D, HEADS * HD), D ** -0.5, 0.109375, ((0, 4),))
    ref_wv = scatter_about(keys[5], (D, HEADS * HD), D ** -0.5, 0.109375, ((0, 4),))
    key_gain = jnp.clip(jax.random.uniform(keys[6], (HD,), jnp.float32, 1.0, 2.0), 1.0, 2.0)
    return dict(q_tok=q_tok, k_tok=k_tok, v_tok=v_tok, ref_hidden=ref_hidden, ref_wk=ref_wk, ref_wv=ref_wv, key_gain=key_gain)


EPSILON = 1e-06

def project_reference(ref_hidden, ref_wk, ref_wv, key_gain):
    k_full = jnp.dot(ref_hidden, ref_wk, preferred_element_type=jnp.float32)
    v_full = jnp.dot(ref_hidden, ref_wv, preferred_element_type=jnp.float32)
    row_count = k_full.shape[0]
    raw_keys = k_full.reshape(row_count, HEADS, HD)
    normed = raw_keys * lax.rsqrt(lax.optimization_barrier(jnp.mean(raw_keys * raw_keys, axis=2, keepdims=True)) + EPSILON) * key_gain
    return (normed.reshape(row_count, HEADS * HD).astype(jnp.bfloat16), v_full.astype(jnp.bfloat16))

def reference(q_tok, k_tok, v_tok, ref_hidden, ref_wk, ref_wv, key_gain):
    ref_keys, ref_vals = project_reference(ref_hidden, ref_wk, ref_wv, key_gain)
    view_count = TOKENS // VIEW_LEN
    factor = HD ** (-0.5)

    def one_view(view_index):
        start_row = (view_index * VIEW_LEN).astype(jnp.int32)
        queries = lax.dynamic_slice_in_dim(q_tok, start_row, VIEW_LEN, 0)
        key_rows = jnp.concatenate((lax.dynamic_slice_in_dim(k_tok, start_row, VIEW_LEN, 0), ref_keys), axis=0)
        val_rows = jnp.concatenate((lax.dynamic_slice_in_dim(v_tok, start_row, VIEW_LEN, 0), ref_vals), axis=0)
        outputs = []
        for head_index in range(HEADS):
            col_start = head_index * HD
            col_stop = col_start + HD
            scores = jnp.dot(queries[:, col_start:col_stop], key_rows[:, col_start:col_stop].T, preferred_element_type=jnp.float32) * factor
            row_max = lax.optimization_barrier(jnp.max(scores, axis=1, keepdims=True))
            weights = jnp.exp(scores - row_max)
            row_total = lax.optimization_barrier(jnp.sum(weights, axis=1, keepdims=True))
            mixed_rows = jnp.dot(weights.astype(jnp.bfloat16), val_rows[:, col_start:col_stop], preferred_element_type=jnp.float32) / row_total
            outputs.append(mixed_rows.astype(jnp.bfloat16))
        return jnp.concatenate(outputs, axis=1)
    blocks = lax.map(one_view, jnp.arange(view_count, dtype=jnp.int32))
    return blocks.reshape(TOKENS, HEADS * HD)
```

```python
import functools

import jax
import jax.numpy as jnp
from jax import lax
from jax.experimental import pallas as pl
from jax.experimental.pallas import tpu as pltpu
from jax.sharding import Mesh
from jax.sharding import PartitionSpec as P

HD = 128
HEADS_HERE = 3
WIDTH = HEADS_HERE * HD
EPSILON = 1e-06
FACTOR = HD**-0.5 * 1.4426950408889634
SEQ = ("x", "w", "y", "core")


def ring(count, shift):
    return [(i, (i + shift) % count) for i in range(count)]


def project_kernel(me_ref, hidden, wk, wv, own, first, second, third):
    step = pl.program_id(0)
    rows = hidden[...]
    k_part = jnp.dot(rows, wk[...], preferred_element_type=jnp.float32)
    v_part = jnp.dot(rows, wv[...], preferred_element_type=jnp.float32)

    @pl.when(step == 3)
    def _():
        own[:, :WIDTH] = k_part
        own[:, WIDTH:] = v_part

    for index, out in ((0, second), (1, first), (2, third)):

        @pl.when(step == index)
        def _():
            out[:, :WIDTH] = k_part.astype(jnp.bfloat16)
            out[:, WIDTH:] = v_part.astype(jnp.bfloat16)


def project(me, hidden, wk, wv):
    rows, depth = hidden.shape
    ahead = (2, 1, 3, 0)

    def group(step, me_ref):
        shift = jnp.where(step == 0, 2, jnp.where(step == 1, 1, jnp.where(step == 2, 3, 0)))
        return (0, lax.rem(me_ref[0] + shift, 4))

    del ahead
    whole = lambda step, me_ref: (0, 0)
    sent = jax.ShapeDtypeStruct((rows, 2 * WIDTH), jnp.bfloat16)
    return pl.pallas_call(
        project_kernel,
        out_shape=(jax.ShapeDtypeStruct((rows, 2 * WIDTH), jnp.float32), sent, sent, sent),
        grid_spec=pltpu.PrefetchScalarGridSpec(
            num_scalar_prefetch=1,
            grid=(4,),
            in_specs=[
                pl.BlockSpec((rows, depth), whole),
                pl.BlockSpec((depth, WIDTH), group),
                pl.BlockSpec((depth, WIDTH), group),
            ],
            out_specs=[pl.BlockSpec((rows, 2 * WIDTH), whole)] * 4,
        ),
        compiler_params=pltpu.CompilerParams(vmem_limit_bytes=32 << 20),
        cost_estimate=pl.CostEstimate(
            flops=2 * rows * depth * 8 * WIDTH, bytes_accessed=2 * depth * 8 * WIDTH, transcendentals=0
        ),
        name="project",
    )(me, hidden, wk, wv)


def norm_kernel(own, a, b, c, gain, out):
    total = (
        own[...]
        + a[...].astype(jnp.float32)
        + b[...].astype(jnp.float32)
        + c[...].astype(jnp.float32)
    )
    for head in range(HEADS_HERE):
        cols = slice(head * HD, (head + 1) * HD)
        raw = total[:, cols]
        scale = lax.rsqrt(jnp.mean(raw * raw, axis=1, keepdims=True) + EPSILON)
        out[:, cols] = (raw * scale * gain[...]).astype(jnp.bfloat16)
    out[:, WIDTH:] = total[:, WIDTH:].astype(jnp.bfloat16)


def norm(own, a, b, c, gain):
    rows = own.shape[0]
    return pl.pallas_call(
        norm_kernel,
        out_shape=jax.ShapeDtypeStruct((rows, 2 * WIDTH), jnp.bfloat16),
        cost_estimate=pl.CostEstimate(flops=10 * own.size, bytes_accessed=12 * own.size, transcendentals=128),
        name="norm",
    )(own, a, b, c, gain)


def attend_block(q, kv, acc, top, total, fresh):
    for head in range(HEADS_HERE):
        cols = slice(head * HD, (head + 1) * HD)
        vals = slice(WIDTH + head * HD, WIDTH + (head + 1) * HD)
        scores = lax.dot_general(
            q[:, cols], kv[:, cols], (((1,), (1,)), ((), ())), preferred_element_type=jnp.float32
        )
        high = jnp.max(scores, axis=1, keepdims=True) * FACTOR
        if fresh:
            raised = high
        else:
            old = top[:, head : head + 1]
            raised = jnp.maximum(old, high)
        weights = jnp.exp2(scores * FACTOR - raised)
        row_sum = jnp.sum(weights, axis=1, keepdims=True)
        mixed = jnp.dot(
            weights.astype(jnp.bfloat16), kv[:, vals], preferred_element_type=jnp.float32
        )
        if fresh:
            total[:, head : head + 1] = row_sum
            acc[:, cols] = mixed
        else:
            rescale = jnp.exp2(old - raised)
            total[:, head : head + 1] = total[:, head : head + 1] * rescale + row_sum
            acc[:, cols] = acc[:, cols] * rescale + mixed
        top[:, head : head + 1] = raised


def view_kernel(q, kv, acc, top, total):
    first = pl.program_id(0) == 0

    @pl.when(first)
    def _():
        attend_block(q, kv, acc, top, total, True)

    @pl.when(jnp.logical_not(first))
    def _():
        attend_block(q, kv, acc, top, total, False)


def attend_cost(rows, keys):
    pairs = rows * keys * HEADS_HERE
    return pl.CostEstimate(
        flops=4 * HD * pairs, bytes_accessed=4 * keys * WIDTH + 8 * rows * WIDTH, transcendentals=pairs
    )


def attend_view(q, kv, chunk=1024):
    rows = q.shape[0]
    whole = lambda i: (0, 0)
    return pl.pallas_call(
        view_kernel,
        out_shape=(
            jax.ShapeDtypeStruct((rows, WIDTH), jnp.float32),
            jax.ShapeDtypeStruct((rows, HD), jnp.float32),
            jax.ShapeDtypeStruct((rows, HD), jnp.float32),
        ),
        grid=(kv.shape[0] // chunk,),
        in_specs=[pl.BlockSpec((rows, WIDTH), whole), pl.BlockSpec((chunk, 2 * WIDTH), lambda i: (i, 0))],
        out_specs=[
            pl.BlockSpec((rows, WIDTH), whole),
            pl.BlockSpec((rows, HD), whole),
            pl.BlockSpec((rows, HD), whole),
        ],
        compiler_params=pltpu.CompilerParams(vmem_limit_bytes=48 << 20),
        cost_estimate=attend_cost(rows, kv.shape[0]),
        name="attend_view",
    )(q, kv)


def more_kernel(count, last, q, *refs):
    pieces, (acc_in, top_in, total_in), rest = refs[:count], refs[count : count + 3], refs[count + 3 :]
    if last:
        out, acc, top, total = rest
    else:
        acc, top, total = rest
    acc[...] = acc_in[...]
    top[...] = top_in[...]
    total[...] = total_in[...]
    for piece in pieces:
        attend_block(q, piece, acc, top, total, False)
    if last:
        for head in range(HEADS_HERE):
            cols = slice(head * HD, (head + 1) * HD)
            out[:, cols] = (acc[:, cols] / total[:, head : head + 1]).astype(jnp.bfloat16)


def attend_more(q, pieces, carried, last):
    rows = q.shape[0]
    state = [
        jax.ShapeDtypeStruct((rows, WIDTH), jnp.float32),
        jax.ShapeDtypeStruct((rows, HD), jnp.float32),
        jax.ShapeDtypeStruct((rows, HD), jnp.float32),
    ]
    vmem = pl.BlockSpec(memory_space=pltpu.VMEM)
    if last:
        out_shape, scratch = (
            jax.ShapeDtypeStruct((rows, WIDTH), jnp.bfloat16),
            [pltpu.VMEM(s.shape, s.dtype) for s in state],
        )
        out_specs = vmem
    else:
        out_shape, scratch, out_specs = tuple(state), [], (vmem,) * 3
    return pl.pallas_call(
        functools.partial(more_kernel, len(pieces), last),
        out_shape=out_shape,
        in_specs=[vmem] * (4 + len(pieces)),
        out_specs=out_specs,
        scratch_shapes=scratch,
        compiler_params=pltpu.CompilerParams(vmem_limit_bytes=48 << 20),
        cost_estimate=attend_cost(rows, sum(p.shape[0] for p in pieces)),
        name="attend_last" if last else "attend_more",
    )(q, *pieces, *carried)


def per_device(q_tok, k_tok, v_tok, ref_hidden, ref_wk, ref_wv, key_gain):
    view = lax.all_gather(jnp.concatenate((k_tok, v_tok), axis=1), ("y", "core"), axis=0, tiled=True)

    me = lax.axis_index("tensor").astype(jnp.int32).reshape(1)
    own, *sent = project(me, ref_hidden, ref_wk, ref_wv)
    arrived = [lax.ppermute(block, "tensor", ring(4, shift)) for shift, block in zip((1, 2, 3), sent)]
    block = norm(own, *arrived, key_gain.reshape(1, HD))
    block = jnp.concatenate((block, lax.ppermute(block, "w", ring(2, 1))), axis=0)
    block = jnp.concatenate([block] + [lax.ppermute(block, "y", ring(4, s)) for s in (1, 3, 2)], axis=0)
    pieces = [block] + [lax.ppermute(block, "x", ring(4, s)) for s in (1, 3, 2)]
    others = [lax.ppermute(piece, "core", ring(2, 1)) for piece in pieces]

    carried = attend_view(q_tok, view)
    carried = attend_more(q_tok, pieces, carried, False)
    return attend_more(q_tok, others, carried, True)


def solution(mesh):
    fine = Mesh(
        mesh.devices.reshape(4, 2, 4, 2, 4),
        ("x", "w", "y", "core", "tensor"),
    )
    placed = (
        P(SEQ, "tensor"),
        P(SEQ, "tensor"),
        P(SEQ, "tensor"),
        P(SEQ, "tensor"),
        P("tensor", None),
        P("tensor", None),
        P(),
    )
    return jax.shard_map(
        per_device, mesh=fine, in_specs=placed, out_specs=P(SEQ, "tensor"), check_vma=False
    )
```

```python
import functools

import jax
import jax.numpy as jnp
from jax import lax
from jax.experimental import pallas as pl
from jax.experimental.pallas import tpu as pltpu
from jax.sharding import Mesh
from jax.sharding import PartitionSpec as P

HD = 128
HEADS_HERE = 3
WIDTH = HEADS_HERE * HD
EPSILON = 1e-06
FACTOR = HD**-0.5 * 1.4426950408889634
SEQ = ("x", "w", "y", "core")


def ring(count, shift):
    return [(i, (i + shift) % count) for i in range(count)]


def project_kernel(me_ref, hidden, wk, wv, own, first, second, third):
    step = pl.program_id(0)
    rows = hidden[...]
    k_part = jnp.dot(rows, wk[...], preferred_element_type=jnp.float32)
    v_part = jnp.dot(rows, wv[...], preferred_element_type=jnp.float32)

    @pl.when(step == 3)
    def _():
        own[:, :WIDTH] = k_part
        own[:, WIDTH:] = v_part

    for index, out in ((0, second), (1, first), (2, third)):

        @pl.when(step == index)
        def _():
            out[:, :WIDTH] = k_part.astype(jnp.bfloat16)
            out[:, WIDTH:] = v_part.astype(jnp.bfloat16)


def project(me, hidden, wk, wv):
    rows, depth = hidden.shape
    def group(step, me_ref):
        shift = jnp.where(step == 0, 2, jnp.where(step == 1, 1, jnp.where(step == 2, 3, 0)))
        return (0, lax.rem(me_ref[0] + shift, 4))

    whole = lambda step, me_ref: (0, 0)
    sent = jax.ShapeDtypeStruct((rows, 2 * WIDTH), jnp.bfloat16)
    return pl.pallas_call(
        project_kernel,
        out_shape=(jax.ShapeDtypeStruct((rows, 2 * WIDTH), jnp.float32), sent, sent, sent),
        grid_spec=pltpu.PrefetchScalarGridSpec(
            num_scalar_prefetch=1,
            grid=(4,),
            in_specs=[
                pl.BlockSpec((rows, depth), whole),
                pl.BlockSpec((depth, WIDTH), group),
                pl.BlockSpec((depth, WIDTH), group),
            ],
            out_specs=[pl.BlockSpec((rows, 2 * WIDTH), whole)] * 4,
        ),
        compiler_params=pltpu.CompilerParams(vmem_limit_bytes=8 << 20),
        cost_estimate=pl.CostEstimate(
            flops=2 * rows * depth * 8 * WIDTH, bytes_accessed=2 * depth * 8 * WIDTH, transcendentals=0
        ),
        name="project",
    )(me, hidden, wk, wv)


def norm_kernel(own, a, b, c, gain, out):
    total = (
        own[...]
        + a[...].astype(jnp.float32)
        + b[...].astype(jnp.float32)
        + c[...].astype(jnp.float32)
    )
    for head in range(HEADS_HERE):
        cols = slice(head * HD, (head + 1) * HD)
        raw = total[:, cols]
        scale = lax.rsqrt(jnp.mean(raw * raw, axis=1, keepdims=True) + EPSILON)
        out[:, cols] = (raw * scale * gain[...]).astype(jnp.bfloat16)
    out[:, WIDTH:] = total[:, WIDTH:].astype(jnp.bfloat16)


def norm(own, a, b, c, gain):
    rows = own.shape[0]
    return pl.pallas_call(
        norm_kernel,
        out_shape=jax.ShapeDtypeStruct((rows, 2 * WIDTH), jnp.bfloat16),
        compiler_params=pltpu.CompilerParams(vmem_limit_bytes=2 << 20),
        cost_estimate=pl.CostEstimate(flops=10 * own.size, bytes_accessed=12 * own.size, transcendentals=128),
        name="norm",
    )(own, a, b, c, gain)


def attend_kernel(moves, keys, chunk, block, fresh, q, *refs):
    operands = 1 + max(move[0] for move in moves)
    pieces, refs = refs[:operands], refs[operands:]
    if not fresh:
        carried, refs = refs[0], refs[1:]
    out, held, sems = refs
    copies = []
    for index, (operand, source, count, row, col, width) in enumerate(moves):
        copy = pltpu.make_async_copy(
            pieces[operand].at[pl.ds(source, count), :],
            held.at[pl.ds(row, count), pl.ds(col, width)],
            sems.at[index],
        )
        copy.start()
        copies.append((row, copy))
    ones = jnp.ones((chunk, HD), jnp.bfloat16)
    rows = q.shape[0]
    state = {}
    for base in range(0, keys, chunk):
        for begin, copy in copies:
            if base <= begin < base + chunk:
                copy.wait()
        for low in range(0, rows, block):
            here = slice(low, low + block)
            for head in range(HEADS_HERE):
                cols = slice(head * HD, (head + 1) * HD)
                vals = slice(WIDTH + head * HD, WIDTH + (head + 1) * HD)
                top_at = slice(WIDTH + head, WIDTH + head + 1)
                sum_at = slice(WIDTH + HEADS_HERE + head, WIDTH + HEADS_HERE + head + 1)
                if base:
                    old = state[low, head]
                elif fresh:
                    old = None
                else:
                    old = (carried[here, top_at], carried[here, sum_at], carried[here, cols])
                scores = lax.dot_general(
                    q[here, cols],
                    held[base : base + chunk, cols],
                    (((1,), (1,)), ((), ())),
                    preferred_element_type=jnp.float32,
                )
                raised = jnp.max(scores, axis=1, keepdims=True) * FACTOR
                if old is not None:
                    raised = jnp.maximum(raised, old[0])
                weights = jnp.exp2(scores * FACTOR - raised).astype(jnp.bfloat16)
                mixed = jnp.dot(
                    weights,
                    jnp.concatenate((held[base : base + chunk, vals], ones), axis=1),
                    preferred_element_type=jnp.float32,
                )
                acc, total = mixed[:, :HD], mixed[:, HD:]
                if old is not None:
                    rescale = jnp.exp2(old[0] - raised)
                    acc = old[2] * rescale + acc
                    total = old[1] * rescale + total
                state[low, head] = (raised, total, acc)
                if base + chunk >= keys:
                    out[here, cols] = acc
                    out[here, top_at] = raised
                    out[here, sum_at] = total[:, :1]


def attend(q, pieces, moves, carried=None, chunk=1024, block=256):
    rows = q.shape[0]
    keys = max(move[2] + move[3] for move in moves)
    chunk = min(chunk, keys)
    vmem, anywhere = pl.BlockSpec(memory_space=pltpu.VMEM), pl.BlockSpec(memory_space=pl.ANY)
    carried = () if carried is None else (carried,)
    pairs = rows * keys * HEADS_HERE
    return pl.pallas_call(
        functools.partial(attend_kernel, moves, keys, chunk, block, not carried),
        out_shape=jax.ShapeDtypeStruct((rows, WIDTH + HD), jnp.float32),
        in_specs=[vmem] + [anywhere] * len(pieces) + [vmem] * len(carried),
        out_specs=vmem,
        scratch_shapes=[
            pltpu.VMEM((keys, 2 * WIDTH), jnp.bfloat16),
            pltpu.SemaphoreType.DMA((len(moves),)),
        ],
        compiler_params=pltpu.CompilerParams(vmem_limit_bytes=20 << 20),
        cost_estimate=pl.CostEstimate(
            flops=4 * HD * pairs,
            bytes_accessed=4 * keys * WIDTH + 8 * rows * WIDTH,
            transcendentals=pairs,
        ),
        name="attend_more" if carried else "attend_view",
    )(q, *pieces, *carried)


def join_kernel(a, b, out):
    for head in range(HEADS_HERE):
        cols = slice(head * HD, (head + 1) * HD)
        top_at = slice(WIDTH + head, WIDTH + head + 1)
        sum_at = slice(WIDTH + HEADS_HERE + head, WIDTH + HEADS_HERE + head + 1)
        top_a, top_b = a[:, top_at], b[:, top_at]
        top = jnp.maximum(top_a, top_b)
        scale_a, scale_b = jnp.exp2(top_a - top), jnp.exp2(top_b - top)
        total = a[:, sum_at] * scale_a + b[:, sum_at] * scale_b
        out[:, cols] = ((a[:, cols] * scale_a + b[:, cols] * scale_b) / total).astype(jnp.bfloat16)


def join(a, b):
    return pl.pallas_call(
        join_kernel,
        out_shape=jax.ShapeDtypeStruct((a.shape[0], WIDTH), jnp.bfloat16),
        compiler_params=pltpu.CompilerParams(vmem_limit_bytes=8 << 20),
        cost_estimate=pl.CostEstimate(flops=6 * a.size, bytes_accessed=10 * a.size, transcendentals=6 * a.shape[0]),
        name="join",
    )(a, b)


def hop(block, axis, shift):
    return lax.ppermute(block, axis, ring(2 if axis in ("w", "core") else 4, shift))


def per_device(q_tok, k_tok, v_tok, ref_hidden, ref_wk, ref_wv, key_gain):
    rows = q_tok.shape[0]
    q_peer = hop(q_tok, "core", 1)
    k_back, v_ahead = hop(k_tok, "y", 1), hop(v_tok, "y", 3)
    k_ahead, v_back = hop(k_tok, "y", 3), hop(v_tok, "y", 1)
    ref_hidden, q_peer = lax.optimization_barrier((ref_hidden, q_peer))
    ref_wk, ref_wv = [pltpu.with_memory_space_constraint(w, pltpu.HBM) for w in (ref_wk, ref_wv)]

    me = lax.axis_index("tensor").astype(jnp.int32).reshape(1)
    own, *sent = project(me, ref_hidden, ref_wk, ref_wv)
    arrived = [hop(block, "tensor", shift) for shift, block in zip((1, 2, 3), sent)]
    arrived, k_back, v_ahead = lax.optimization_barrier((arrived, k_back, v_ahead))
    opposite = [hop(k_back, "y", 1), hop(v_ahead, "y", 3)]

    block = norm(own, *arrived, key_gain.reshape(1, HD))
    paired = hop(block, "w", 1)
    paired, k_ahead, v_back = lax.optimization_barrier((paired, k_ahead, v_back))
    block = jnp.concatenate((block, paired), axis=0)
    pieces = [block] + [hop(block, "x", s) for s in (1, 3, 2)]
    pieces, opposite = lax.optimization_barrier((pieces, opposite))
    block = jnp.concatenate(pieces, axis=0)
    pieces = [block] + [hop(block, "y", s) for s in (1, 3, 2)]

    view = [k_tok, v_tok, k_back, v_back, k_ahead, v_ahead] + opposite
    moves = [(i, 0, rows, i // 2 * rows, i % 2 * WIDTH, WIDTH) for i in range(8)]
    at_peer = attend(q_peer, view, moves)
    at_own = attend(q_tok, view, moves)
    pieces, at_peer, at_own = lax.optimization_barrier((pieces, at_peer, at_own))
    size = block.shape[0]
    moves = [(i, 0, size, i * size, 0, 2 * WIDTH) for i in range(4)]
    at_peer = attend(q_peer, pieces, moves, at_peer)
    from_peer = hop(at_peer, "core", 1)
    return join(attend(q_tok, pieces, moves, at_own), from_peer)


def solution(mesh):
    fine = Mesh(
        mesh.devices.reshape(4, 2, 4, 2, 4),
        ("x", "w", "y", "core", "tensor"),
    )
    placed = (
        P(SEQ, "tensor"),
        P(SEQ, "tensor"),
        P(SEQ, "tensor"),
        P(SEQ, "tensor"),
        P("tensor", None),
        P("tensor", None),
        P(),
    )
    return jax.shard_map(
        per_device, mesh=fine, in_specs=placed, out_specs=P(SEQ, "tensor"), check_vma=False
    )
```

```python
import functools

import jax
import jax.numpy as jnp
from jax import lax
from jax.experimental import pallas as pl
from jax.experimental.pallas import tpu as pltpu
from jax.sharding import Mesh
from jax.sharding import PartitionSpec as P

HD = 128
HEADS_HERE = 3
WIDTH = HEADS_HERE * HD
EPSILON = 1e-06
FACTOR = HD**-0.5 * 1.4426950408889634
SEQ = ("x", "w", "y", "core")
SMALL, BULK = "y", "x"


def ring(count, shift):
    return [(i, (i + shift) % count) for i in range(count)]


def project_kernel(hidden, wk, wv, k_tok, v_tok, own, near, far, next_to, beside, rows, weights, sems):
    me = lax.axis_index("tensor")
    first = pltpu.make_async_copy(hidden, rows, sems.at[8])
    first.start()
    copies = []
    for place, ahead in enumerate((1, 2, 3, 0)):
        peer = lax.rem(me + ahead, 4)
        cols = pl.ds(pl.multiple_of(peer * WIDTH, WIDTH), WIDTH)
        for half, source in enumerate((wk, wv)):
            slot = 2 * place + half
            copy = pltpu.make_async_copy(source.at[:, cols], weights.at[slot], sems.at[slot])
            copy.start()
            copies.append(copy)
    sides = []
    for half, source in enumerate((k_tok, v_tok)):
        copy = pltpu.make_async_copy(source, beside.at[:, pl.ds(half * WIDTH, WIDTH)], sems.at[9 + half])
        copy.start()
        sides.append(copy)
    first.wait()
    for place, out in enumerate((near, far, next_to, own)):
        for half in range(2):
            slot = 2 * place + half
            copies[slot].wait()
            part = jnp.dot(rows[...], weights[slot], preferred_element_type=jnp.float32)
            out[:, half * WIDTH : (half + 1) * WIDTH] = part.astype(out.dtype)
    for copy in sides:
        copy.wait()


def project(hidden, wk, wv, k_tok, v_tok):
    rows, depth = hidden.shape
    sent = jax.ShapeDtypeStruct((rows, 2 * WIDTH), jnp.bfloat16)
    vmem, anywhere = pl.BlockSpec(memory_space=pltpu.VMEM), pl.BlockSpec(memory_space=pl.ANY)
    return pl.pallas_call(
        project_kernel,
        out_shape=(
            jax.ShapeDtypeStruct((rows, 2 * WIDTH), jnp.float32),
            sent,
            sent,
            sent,
            jax.ShapeDtypeStruct((k_tok.shape[0], 2 * WIDTH), jnp.bfloat16),
        ),
        in_specs=[anywhere] * 5,
        out_specs=(vmem,) * 4 + (anywhere,),
        scratch_shapes=[
            pltpu.VMEM((rows, depth), jnp.bfloat16),
            pltpu.VMEM((8, depth, WIDTH), jnp.bfloat16),
            pltpu.SemaphoreType.DMA((11,)),
        ],
        compiler_params=pltpu.CompilerParams(vmem_limit_bytes=8 << 20),
        cost_estimate=pl.CostEstimate(
            flops=2 * rows * depth * 8 * WIDTH, bytes_accessed=2 * depth * 8 * WIDTH, transcendentals=0
        ),
        name="project",
    )(hidden, wk, wv, k_tok, v_tok)


def norm_kernel(own, a, b, c, gain, out):
    total = (
        own[...]
        + a[...].astype(jnp.float32)
        + b[...].astype(jnp.float32)
        + c[...].astype(jnp.float32)
    )
    for head in range(HEADS_HERE):
        cols = slice(head * HD, (head + 1) * HD)
        raw = total[:, cols]
        scale = lax.rsqrt(jnp.mean(raw * raw, axis=1, keepdims=True) + EPSILON)
        out[:, cols] = (raw * scale * gain[...]).astype(jnp.bfloat16)
    out[:, WIDTH:] = total[:, WIDTH:].astype(jnp.bfloat16)


def norm(own, a, b, c, gain):
    rows = own.shape[0]
    return pl.pallas_call(
        norm_kernel,
        out_shape=jax.ShapeDtypeStruct((rows, 2 * WIDTH), jnp.bfloat16),
        compiler_params=pltpu.CompilerParams(vmem_limit_bytes=2 << 20),
        cost_estimate=pl.CostEstimate(flops=10 * own.size, bytes_accessed=12 * own.size, transcendentals=128),
        name="norm",
    )(own, a, b, c, gain)


def attend_kernel(moves, keys, chunk, block, count_q, *refs):
    operands = 1 + max(move[0] for move in moves)
    queries, refs = refs[:count_q], refs[count_q:]
    pieces, refs = refs[:operands], refs[operands:]
    outs, (held, sems) = refs[:count_q], refs[count_q:]
    copies = []
    for index, (operand, source, count, row, col, width) in enumerate(moves):
        copy = pltpu.make_async_copy(
            pieces[operand].at[pl.ds(source, count), :],
            held.at[pl.ds(row, count), pl.ds(col, width)],
            sems.at[index],
        )
        copy.start()
        copies.append((row, copy))
    ones = jnp.ones((chunk, HD), jnp.bfloat16)
    rows = queries[0].shape[0]
    state = {}
    for base in range(0, keys, chunk):
        for begin, copy in copies:
            if base <= begin < base + chunk:
                copy.wait()
        for which, low in [(which, low) for which in range(count_q) for low in range(0, rows, block)]:
            q, out = queries[which], outs[which]
            here = slice(low, low + block)
            for head in range(HEADS_HERE):
                cols = slice(head * HD, (head + 1) * HD)
                vals = slice(WIDTH + head * HD, WIDTH + (head + 1) * HD)
                old = state.get((which, low, head))
                scores = lax.dot_general(
                    q[here, cols],
                    held[base : base + chunk, cols],
                    (((1,), (1,)), ((), ())),
                    preferred_element_type=jnp.float32,
                )
                raised = jnp.max(scores, axis=1, keepdims=True) * FACTOR
                if old is not None:
                    raised = jnp.maximum(raised, old[0])
                weights = jnp.exp2(scores * FACTOR - raised).astype(jnp.bfloat16)
                mixed = jnp.dot(
                    weights,
                    jnp.concatenate((held[base : base + chunk, vals], ones), axis=1),
                    preferred_element_type=jnp.float32,
                )
                acc, total = mixed[:, :HD], mixed[:, HD:]
                if old is not None:
                    rescale = jnp.exp2(old[0] - raised)
                    acc = old[2] * rescale + acc
                    total = old[1] * rescale + total
                state[which, low, head] = (raised, total, acc)
                if base + chunk >= keys:
                    if head == 0:
                        out[here, WIDTH:] = jnp.zeros((block, HD), jnp.float32)
                    out[here, cols] = acc
                    out[here, WIDTH + head : WIDTH + head + 1] = raised
                    out[here, WIDTH + HEADS_HERE + head : WIDTH + HEADS_HERE + head + 1] = total[:, :1]


def attend(queries, pieces, moves, chunk=1024, block=256):
    rows = queries[0].shape[0]
    keys = max(move[2] + move[3] for move in moves)
    chunk = min(chunk, keys)
    vmem, anywhere = pl.BlockSpec(memory_space=pltpu.VMEM), pl.BlockSpec(memory_space=pl.ANY)
    return pl.pallas_call(
        functools.partial(attend_kernel, moves, keys, chunk, block, len(queries)),
        out_shape=(jax.ShapeDtypeStruct((rows, WIDTH + HD), jnp.float32),) * len(queries),
        in_specs=[vmem] * len(queries) + [anywhere] * len(pieces),
        out_specs=(vmem,) * len(queries),
        scratch_shapes=[
            pltpu.VMEM((keys, 2 * WIDTH), jnp.bfloat16),
            pltpu.SemaphoreType.DMA((len(moves),)),
        ],
        compiler_params=pltpu.CompilerParams(vmem_limit_bytes=20 << 20),
        name="attend",
    )(*queries, *pieces)


def join_kernel(last, *refs):
    *parts, out = refs
    stats = [part[:, WIDTH:] for part in parts]
    top = functools.reduce(jnp.maximum, stats)
    scales = [jnp.exp2(stat - top) for stat in stats]
    total = sum(pltpu.roll(stat, HD - HEADS_HERE, axis=1) * scale for stat, scale in zip(stats, scales))
    if last:
        scales = [scale / total for scale in scales]
    else:
        out[:, WIDTH:] = jnp.zeros((top.shape[0], HD), jnp.float32)
        out[:, WIDTH : WIDTH + HEADS_HERE] = top[:, :HEADS_HERE]
        out[:, WIDTH + HEADS_HERE : WIDTH + 2 * HEADS_HERE] = total[:, :HEADS_HERE]
    for head in range(HEADS_HERE):
        cols = slice(head * HD, (head + 1) * HD)
        out[:, cols] = sum(
            part[:, cols] * scale[:, head : head + 1] for part, scale in zip(parts, scales)
        ).astype(out.dtype)


def join(parts, last):
    rows = parts[0].shape[0]
    size = parts[0].size
    return pl.pallas_call(
        functools.partial(join_kernel, last),
        out_shape=jax.ShapeDtypeStruct((rows, WIDTH), jnp.bfloat16)
        if last
        else jax.ShapeDtypeStruct(parts[0].shape, jnp.float32),
        compiler_params=pltpu.CompilerParams(vmem_limit_bytes=8 << 20),
        cost_estimate=pl.CostEstimate(
            flops=3 * len(parts) * size, bytes_accessed=4 * len(parts) * size, transcendentals=HD * rows
        ),
        name="join_last" if last else "join",
    )(*parts)


def hop(block, axis, shift):
    return lax.ppermute(block, axis, ring(2 if axis in ("w", "core") else 4, shift))


def per_device(q_tok, k_tok, v_tok, ref_hidden, ref_wk, ref_wv, key_gain):
    rows = q_tok.shape[0]
    barrier = lax.optimization_barrier
    inputs = [pltpu.with_memory_space_constraint(a, pltpu.HBM) for a in (ref_hidden, ref_wk, ref_wv, k_tok, v_tok)]
    own, *sent, beside = project(*inputs)
    arrived = [hop(block, "tensor", shift) for shift, block in zip((1, 2, 3), sent)]
    back, ahead = hop(beside, "y", 1), hop(beside, "y", 3)

    block = norm(own, *arrived, key_gain.reshape(1, HD))
    paired, q_peer = barrier((hop(block, "w", 1), hop(q_tok, "core", 1)))
    block = jnp.concatenate((block, paired), axis=0)
    pieces = [block] + [hop(block, SMALL, s) for s in (1, 3, 2)]
    pieces, back, ahead = barrier((pieces, back, ahead))
    block = jnp.concatenate(pieces, axis=0)
    late = [hop(block, BULK, s) for s in (1, 3, 2)]
    half = rows // 2
    opposite = [hop(back[:half], "y", 1), hop(ahead[half:], "y", 3)]

    moves = [(i, 0, rows, i * rows, 0, 2 * WIDTH) for i in range(2)]
    peer_a, own_a = attend((q_peer, q_tok), (beside, back), moves)
    opposite, peer_a, own_a = barrier((opposite, peer_a, own_a))
    moves = [(0, 0, rows, 0, 0, 2 * WIDTH)]
    moves += [(1 + i, 0, half, rows + i * half, 0, 2 * WIDTH) for i in range(2)]
    peer_b, own_b = attend((q_peer, q_tok), [ahead] + opposite, moves)
    late, peer_b, own_b = barrier((late, peer_b, own_b))
    size = block.shape[0]
    moves = [(i, 0, size, i * size, 0, 2 * WIDTH) for i in range(4)]
    (peer_c,) = attend((q_peer,), [block] + late, moves)
    from_peer = hop(join((peer_a, peer_b, peer_c), False), "core", 1)
    (own_c,) = attend((q_tok,), [block] + late, moves)
    return join((own_a, own_b, own_c, from_peer), True)


def solution(mesh):
    fine = Mesh(
        mesh.devices.reshape(4, 2, 4, 2, 4),
        ("x", "w", "y", "core", "tensor"),
    )
    placed = (
        P(SEQ, "tensor"),
        P(SEQ, "tensor"),
        P(SEQ, "tensor"),
        P(SEQ, "tensor"),
        P("tensor", None),
        P("tensor", None),
        P(),
    )
    return jax.shard_map(
        per_device, mesh=fine, in_specs=placed, out_specs=P(SEQ, "tensor"), check_vma=False
    )
```

```python
import functools

import jax
import jax.numpy as jnp
from jax import lax
from jax.experimental import pallas as pl
from jax.experimental.pallas import tpu as pltpu
from jax.sharding import Mesh
from jax.sharding import PartitionSpec as P

HD = 128
HEADS_HERE = 3
WIDTH = HEADS_HERE * HD
EPSILON = 1e-06
FACTOR = HD**-0.5 * 1.4426950408889634
SEQ = ("x", "w", "y", "core")
SMALL, BULK = "y", "x"


def ring(count, shift):
    return [(i, (i + shift) % count) for i in range(count)]


def project_kernel(hidden, wk, wv, k_tok, v_tok, own, near, far, next_to, beside, rows, weights, sems):
    me = lax.axis_index("tensor")
    first = pltpu.make_async_copy(hidden, rows, sems.at[8])
    first.start()
    copies = []
    for place, ahead in enumerate((1, 2, 3, 0)):
        peer = lax.rem(me + ahead, 4)
        cols = pl.ds(pl.multiple_of(peer * WIDTH, WIDTH), WIDTH)
        for half, source in enumerate((wk, wv)):
            slot = 2 * place + half
            copy = pltpu.make_async_copy(source.at[:, cols], weights.at[slot], sems.at[slot])
            copy.start()
            copies.append(copy)
    sides = []
    for half, source in enumerate((k_tok, v_tok)):
        copy = pltpu.make_async_copy(source, beside.at[:, pl.ds(half * WIDTH, WIDTH)], sems.at[9 + half])
        copy.start()
        sides.append(copy)
    first.wait()
    for place, out in enumerate((near, far, next_to, own)):
        for half in range(2):
            slot = 2 * place + half
            copies[slot].wait()
            part = jnp.dot(rows[...], weights[slot], preferred_element_type=jnp.float32)
            out[:, half * WIDTH : (half + 1) * WIDTH] = part.astype(out.dtype)
    for copy in sides:
        copy.wait()


def project(hidden, wk, wv, k_tok, v_tok):
    rows, depth = hidden.shape
    sent = jax.ShapeDtypeStruct((rows, 2 * WIDTH), jnp.bfloat16)
    vmem, anywhere = pl.BlockSpec(memory_space=pltpu.VMEM), pl.BlockSpec(memory_space=pl.ANY)
    return pl.pallas_call(
        project_kernel,
        out_shape=(
            jax.ShapeDtypeStruct((rows, 2 * WIDTH), jnp.float32),
            sent,
            sent,
            sent,
            jax.ShapeDtypeStruct((k_tok.shape[0], 2 * WIDTH), jnp.bfloat16),
        ),
        in_specs=[anywhere] * 5,
        out_specs=(vmem,) * 4 + (anywhere,),
        scratch_shapes=[
            pltpu.VMEM((rows, depth), jnp.bfloat16),
            pltpu.VMEM((8, depth, WIDTH), jnp.bfloat16),
            pltpu.SemaphoreType.DMA((11,)),
        ],
        compiler_params=pltpu.CompilerParams(vmem_limit_bytes=8 << 20),
        cost_estimate=pl.CostEstimate(
            flops=2 * rows * depth * 8 * WIDTH, bytes_accessed=2 * depth * 8 * WIDTH, transcendentals=0
        ),
        name="project",
    )(hidden, wk, wv, k_tok, v_tok)


def norm_kernel(own, a, b, c, gain, out):
    total = (
        own[...]
        + a[...].astype(jnp.float32)
        + b[...].astype(jnp.float32)
        + c[...].astype(jnp.float32)
    )
    for head in range(HEADS_HERE):
        cols = slice(head * HD, (head + 1) * HD)
        raw = total[:, cols]
        scale = lax.rsqrt(jnp.mean(raw * raw, axis=1, keepdims=True) + EPSILON)
        out[:, cols] = (raw * scale * gain[...]).astype(jnp.bfloat16)
    out[:, WIDTH:] = total[:, WIDTH:].astype(jnp.bfloat16)


def norm(own, a, b, c, gain):
    rows = own.shape[0]
    return pl.pallas_call(
        norm_kernel,
        out_shape=jax.ShapeDtypeStruct((rows, 2 * WIDTH), jnp.bfloat16),
        compiler_params=pltpu.CompilerParams(vmem_limit_bytes=2 << 20),
        cost_estimate=pl.CostEstimate(flops=10 * own.size, bytes_accessed=12 * own.size, transcendentals=128),
        name="norm",
    )(own, a, b, c, gain)


def attend_kernel(moves, keys, chunk, block, count_q, *refs):
    operands = 1 + max(move[0] for move in moves)
    queries, refs = refs[:count_q], refs[count_q:]
    pieces, refs = refs[:operands], refs[operands:]
    outs, (held, sems) = refs[:count_q], refs[count_q:]
    copies = []
    for index, (operand, source, count, row, col, width) in enumerate(moves):
        copy = pltpu.make_async_copy(
            pieces[operand].at[pl.ds(source, count), :],
            held.at[pl.ds(row, count), pl.ds(col, width)],
            sems.at[index],
        )
        copy.start()
        copies.append((row, copy))
    ones = jnp.ones((chunk, HD), jnp.bfloat16)
    rows = queries[0].shape[0]
    state = {}
    for base in range(0, keys, chunk):
        for begin, copy in copies:
            if base <= begin < base + chunk:
                copy.wait()
        for which, low in [(which, low) for which in range(count_q) for low in range(0, rows, block)]:
            q, out = queries[which], outs[which]
            here = slice(low, low + block)
            for head in range(HEADS_HERE):
                cols = slice(head * HD, (head + 1) * HD)
                vals = slice(WIDTH + head * HD, WIDTH + (head + 1) * HD)
                old = state.get((which, low, head))
                scores = lax.dot_general(
                    q[here, cols],
                    held[base : base + chunk, cols],
                    (((1,), (1,)), ((), ())),
                    preferred_element_type=jnp.float32,
                )
                raised = jnp.max(scores, axis=1, keepdims=True) * FACTOR
                if old is not None:
                    raised = jnp.maximum(raised, old[0])
                weights = jnp.exp2(scores * FACTOR - raised).astype(jnp.bfloat16)
                mixed = jnp.dot(
                    weights,
                    jnp.concatenate((held[base : base + chunk, vals], ones), axis=1),
                    preferred_element_type=jnp.float32,
                )
                acc, total = mixed[:, :HD], mixed[:, HD:]
                if old is not None:
                    rescale = jnp.exp2(old[0] - raised)
                    acc = old[2] * rescale + acc
                    total = old[1] * rescale + total
                state[which, low, head] = (raised, total, acc)
                if base + chunk >= keys:
                    if head == 0:
                        out[here, WIDTH:] = jnp.zeros((block, HD), jnp.float32)
                    out[here, cols] = acc
                    out[here, WIDTH + head : WIDTH + head + 1] = raised
                    out[here, WIDTH + HEADS_HERE + head : WIDTH + HEADS_HERE + head + 1] = total[:, :1]


def attend(queries, pieces, moves, chunk=1024, block=256):
    rows = queries[0].shape[0]
    keys = max(move[2] + move[3] for move in moves)
    chunk = min(chunk, keys)
    vmem, anywhere = pl.BlockSpec(memory_space=pltpu.VMEM), pl.BlockSpec(memory_space=pl.ANY)
    return pl.pallas_call(
        functools.partial(attend_kernel, moves, keys, chunk, block, len(queries)),
        out_shape=(jax.ShapeDtypeStruct((rows, WIDTH + HD), jnp.float32),) * len(queries),
        in_specs=[vmem] * len(queries) + [anywhere] * len(pieces),
        out_specs=(vmem,) * len(queries),
        scratch_shapes=[
            pltpu.VMEM((keys, 2 * WIDTH), jnp.bfloat16),
            pltpu.SemaphoreType.DMA((len(moves),)),
        ],
        compiler_params=pltpu.CompilerParams(vmem_limit_bytes=20 << 20),
        name="attend",
    )(*queries, *pieces)


def join_kernel(count, last, *refs):
    outs = refs[-count:]
    each = (len(refs) - count) // count
    for index, out in enumerate(outs):
        join_one(last, refs[index * each : (index + 1) * each], out)


def join_one(last, parts, out):
    stats = [part[:, WIDTH:] for part in parts]
    top = functools.reduce(jnp.maximum, stats)
    scales = [jnp.exp2(stat - top) for stat in stats]
    total = sum(pltpu.roll(stat, HD - HEADS_HERE, axis=1) * scale for stat, scale in zip(stats, scales))
    if last:
        scales = [scale / total for scale in scales]
    else:
        out[:, WIDTH:] = jnp.zeros((top.shape[0], HD), jnp.float32)
        out[:, WIDTH : WIDTH + HEADS_HERE] = top[:, :HEADS_HERE]
        out[:, WIDTH + HEADS_HERE : WIDTH + 2 * HEADS_HERE] = total[:, :HEADS_HERE]
    for head in range(HEADS_HERE):
        cols = slice(head * HD, (head + 1) * HD)
        out[:, cols] = sum(
            part[:, cols] * scale[:, head : head + 1] for part, scale in zip(parts, scales)
        ).astype(out.dtype)


def join(groups, last):
    first = groups[0][0]
    rows = first.shape[0]
    size = sum(part.size for parts in groups for part in parts)
    shape = jax.ShapeDtypeStruct((rows, WIDTH), jnp.bfloat16) if last else jax.ShapeDtypeStruct(first.shape, jnp.float32)
    return pl.pallas_call(
        functools.partial(join_kernel, len(groups), last),
        out_shape=(shape,) * len(groups),
        compiler_params=pltpu.CompilerParams(vmem_limit_bytes=12 << 20),
        cost_estimate=pl.CostEstimate(flops=3 * size, bytes_accessed=4 * size, transcendentals=HD * rows),
        name="join_last" if last else "join",
    )(*[part for parts in groups for part in parts])


def hop(block, axis, shift):
    return lax.ppermute(block, axis, ring(2 if axis in ("w", "core") else 4, shift))


def per_device(q_tok, k_tok, v_tok, ref_hidden, ref_wk, ref_wv, key_gain):
    rows = q_tok.shape[0]
    barrier = lax.optimization_barrier
    inputs = [pltpu.with_memory_space_constraint(a, pltpu.HBM) for a in (ref_hidden, ref_wk, ref_wv, k_tok, v_tok)]
    own, *sent, beside = project(*inputs)
    arrived = [hop(block, "tensor", shift) for shift, block in zip((1, 2, 3), sent)]
    back, ahead = hop(beside, "y", 1), hop(beside, "y", 3)

    block = norm(own, *arrived, key_gain.reshape(1, HD))
    block, q_late = barrier((block, q_tok))
    paired, q_peer = barrier((hop(block, "w", 1), hop(q_late, "core", 1)))
    block = jnp.concatenate((block, paired), axis=0)
    pieces = [block] + [hop(block, SMALL, s) for s in (1, 3, 2)]
    pieces[1], back, ahead = barrier((pieces[1], back, ahead))
    block = jnp.concatenate(pieces, axis=0)
    late = [hop(block, BULK, s) for s in (1, 3, 2)]
    half = rows // 2
    opposite = [hop(back[:half], "y", 1), hop(ahead[half:], "y", 3)]

    moves = [(i, 0, rows, i * rows, 0, 2 * WIDTH) for i in range(2)]
    peer_a, own_a = attend((q_peer, q_tok), (beside, back), moves)
    opposite, peer_a, own_a = barrier((opposite, peer_a, own_a))
    size = block.shape[0]
    moves = [(0, 0, rows, 0, 0, 2 * WIDTH), (1, 0, size, 2 * rows, 0, 2 * WIDTH)]
    moves += [(2 + i, 0, half, rows + i * half, 0, 2 * WIDTH) for i in range(2)]
    peer_b, own_b = attend((q_peer, q_tok), [ahead, block] + opposite, moves, chunk=2 * rows + size)
    peer_ab, own_ab = join(((peer_a, peer_b), (own_a, own_b)), False)
    late, peer_ab, own_ab = barrier((late, peer_ab, own_ab))
    moves = [(i, 0, size, i * size, 0, 2 * WIDTH) for i in range(3)]
    (peer_c,) = attend((q_peer,), late, moves)
    from_peer = hop(*join(((peer_ab, peer_c),), False), "core", 1)
    (own_c,) = attend((q_tok,), late, moves)
    return join(((own_ab, own_c, from_peer),), True)[0]


def solution(mesh):
    fine = Mesh(
        mesh.devices.reshape(4, 2, 4, 2, 4),
        ("x", "w", "y", "core", "tensor"),
    )
    placed = (
        P(SEQ, "tensor"),
        P(SEQ, "tensor"),
        P(SEQ, "tensor"),
        P(SEQ, "tensor"),
        P("tensor", None),
        P("tensor", None),
        P(),
    )
    return jax.shard_map(
        per_device, mesh=fine, in_specs=placed, out_specs=P(SEQ, "tensor"), check_vma=False
    )
```

```python
import functools

import jax
import jax.numpy as jnp
from jax import lax
from jax.experimental import pallas as pl
from jax.experimental.pallas import tpu as pltpu
from jax.sharding import Mesh
from jax.sharding import PartitionSpec as P

HD = 128
HEADS_HERE = 3
WIDTH = HEADS_HERE * HD
EPSILON = 1e-06
FACTOR = HD**-0.5 * 1.4426950408889634
SEQ = ("x", "w", "y", "core")
SMALL, BULK = "y", "x"


def ring(count, shift):
    return [(i, (i + shift) % count) for i in range(count)]


def project_kernel(hidden, wk, wv, k_tok, v_tok, own, near, far, next_to, beside, rows, weights, sems):
    me = lax.axis_index("tensor")
    first = pltpu.make_async_copy(hidden, rows, sems.at[8])
    first.start()
    copies = []
    for place, ahead in enumerate((1, 2, 3, 0)):
        peer = lax.rem(me + ahead, 4)
        cols = pl.ds(pl.multiple_of(peer * WIDTH, WIDTH), WIDTH)
        for half, source in enumerate((wk, wv)):
            slot = 2 * place + half
            copy = pltpu.make_async_copy(source.at[:, cols], weights.at[slot], sems.at[slot])
            copy.start()
            copies.append(copy)
    sides = []
    for half, source in enumerate((k_tok, v_tok)):
        copy = pltpu.make_async_copy(source, beside.at[:, pl.ds(half * WIDTH, WIDTH)], sems.at[9 + half])
        copy.start()
        sides.append(copy)
    first.wait()
    for place, out in enumerate((near, far, next_to, own)):
        for half in range(2):
            slot = 2 * place + half
            copies[slot].wait()
            part = jnp.dot(rows[...], weights[slot], preferred_element_type=jnp.float32)
            out[:, half * WIDTH : (half + 1) * WIDTH] = part.astype(out.dtype)
    for copy in sides:
        copy.wait()


def project(hidden, wk, wv, k_tok, v_tok):
    rows, depth = hidden.shape
    sent = jax.ShapeDtypeStruct((rows, 2 * WIDTH), jnp.bfloat16)
    vmem, anywhere = pl.BlockSpec(memory_space=pltpu.VMEM), pl.BlockSpec(memory_space=pl.ANY)
    return pl.pallas_call(
        project_kernel,
        out_shape=(
            jax.ShapeDtypeStruct((rows, 2 * WIDTH), jnp.float32),
            sent,
            sent,
            sent,
            jax.ShapeDtypeStruct((k_tok.shape[0], 2 * WIDTH), jnp.bfloat16),
        ),
        in_specs=[anywhere] * 5,
        out_specs=(vmem,) * 4 + (anywhere,),
        scratch_shapes=[
            pltpu.VMEM((rows, depth), jnp.bfloat16),
            pltpu.VMEM((8, depth, WIDTH), jnp.bfloat16),
            pltpu.SemaphoreType.DMA((11,)),
        ],
        compiler_params=pltpu.CompilerParams(vmem_limit_bytes=8 << 20),
        cost_estimate=pl.CostEstimate(
            flops=2 * rows * depth * 8 * WIDTH, bytes_accessed=2 * depth * 8 * WIDTH, transcendentals=0
        ),
        name="project",
    )(hidden, wk, wv, k_tok, v_tok)


def norm_kernel(own, a, b, c, gain, out):
    total = (
        own[...]
        + a[...].astype(jnp.float32)
        + b[...].astype(jnp.float32)
        + c[...].astype(jnp.float32)
    )
    for head in range(HEADS_HERE):
        cols = slice(head * HD, (head + 1) * HD)
        raw = total[:, cols]
        scale = lax.rsqrt(jnp.mean(raw * raw, axis=1, keepdims=True) + EPSILON)
        out[:, cols] = (raw * scale * gain[...]).astype(jnp.bfloat16)
    out[:, WIDTH:] = total[:, WIDTH:].astype(jnp.bfloat16)


def norm(own, a, b, c, gain):
    rows = own.shape[0]
    return pl.pallas_call(
        norm_kernel,
        out_shape=jax.ShapeDtypeStruct((rows, 2 * WIDTH), jnp.bfloat16),
        compiler_params=pltpu.CompilerParams(vmem_limit_bytes=2 << 20),
        cost_estimate=pl.CostEstimate(flops=10 * own.size, bytes_accessed=12 * own.size, transcendentals=128),
        name="norm",
    )(own, a, b, c, gain)


def attend_kernel(moves, keys, chunk, block, count_q, *refs):
    operands = 1 + max(move[0] for move in moves)
    queries, refs = refs[:count_q], refs[count_q:]
    pieces, refs = refs[:operands], refs[operands:]
    outs, (held, sems) = refs[:count_q], refs[count_q:]
    copies = []
    for index, (operand, source, count, row, col, width) in enumerate(moves):
        copy = pltpu.make_async_copy(
            pieces[operand].at[pl.ds(source, count), :],
            held.at[pl.ds(row, count), pl.ds(col, width)],
            sems.at[index],
        )
        copy.start()
        copies.append((row, copy))
    ones = jnp.ones((chunk, HD), jnp.bfloat16)
    rows = queries[0].shape[0]
    state = {}
    for base in range(0, keys, chunk):
        for begin, copy in copies:
            if base <= begin < base + chunk:
                copy.wait()
        for which, low in [(which, low) for which in range(count_q) for low in range(0, rows, block)]:
            q, out = queries[which], outs[which]
            here = slice(low, low + block)
            for head in range(HEADS_HERE):
                cols = slice(head * HD, (head + 1) * HD)
                vals = slice(WIDTH + head * HD, WIDTH + (head + 1) * HD)
                old = state.get((which, low, head))
                scores = lax.dot_general(
                    q[here, cols],
                    held[base : base + chunk, cols],
                    (((1,), (1,)), ((), ())),
                    preferred_element_type=jnp.float32,
                )
                raised = jnp.max(scores, axis=1, keepdims=True) * FACTOR
                if old is not None:
                    raised = jnp.maximum(raised, old[0])
                weights = jnp.exp2(scores * FACTOR - raised).astype(jnp.bfloat16)
                mixed = jnp.dot(
                    weights,
                    jnp.concatenate((held[base : base + chunk, vals], ones), axis=1),
                    preferred_element_type=jnp.float32,
                )
                acc, total = mixed[:, :HD], mixed[:, HD:]
                if old is not None:
                    rescale = jnp.exp2(old[0] - raised)
                    acc = old[2] * rescale + acc
                    total = old[1] * rescale + total
                state[which, low, head] = (raised, total, acc)
                if base + chunk >= keys:
                    if head == 0:
                        out[here, WIDTH:] = jnp.zeros((block, HD), jnp.float32)
                    out[here, cols] = acc
                    out[here, WIDTH + head : WIDTH + head + 1] = raised
                    out[here, WIDTH + HEADS_HERE + head : WIDTH + HEADS_HERE + head + 1] = total[:, :1]


def attend(queries, pieces, moves, chunk=1024, block=256):
    rows = queries[0].shape[0]
    keys = max(move[2] + move[3] for move in moves)
    chunk = min(chunk, keys)
    vmem, anywhere = pl.BlockSpec(memory_space=pltpu.VMEM), pl.BlockSpec(memory_space=pl.ANY)
    return pl.pallas_call(
        functools.partial(attend_kernel, moves, keys, chunk, block, len(queries)),
        out_shape=(jax.ShapeDtypeStruct((rows, WIDTH + HD), jnp.float32),) * len(queries),
        in_specs=[vmem] * len(queries) + [anywhere] * len(pieces),
        out_specs=(vmem,) * len(queries),
        scratch_shapes=[
            pltpu.VMEM((keys, 2 * WIDTH), jnp.bfloat16),
            pltpu.SemaphoreType.DMA((len(moves),)),
        ],
        compiler_params=pltpu.CompilerParams(vmem_limit_bytes=20 << 20),
        name="attend",
    )(*queries, *pieces)


def attend_whole_kernel(block, q, *refs):
    *pieces, out = refs
    keys = sum(piece.shape[0] for piece in pieces)
    ones = jnp.ones((keys, HD), jnp.bfloat16)
    for low in range(0, q.shape[0], block):
        here = slice(low, low + block)
        out[here, WIDTH:] = jnp.zeros((block, HD), jnp.float32)
        for head in range(HEADS_HERE):
            cols = slice(head * HD, (head + 1) * HD)
            vals = slice(WIDTH + head * HD, WIDTH + (head + 1) * HD)
            scores = lax.dot_general(
                q[here, cols],
                jnp.concatenate([piece[:, cols] for piece in pieces], axis=0),
                (((1,), (1,)), ((), ())),
                preferred_element_type=jnp.float32,
            )
            raised = jnp.max(scores, axis=1, keepdims=True) * FACTOR
            weights = jnp.exp2(scores * FACTOR - raised).astype(jnp.bfloat16)
            values = jnp.concatenate([piece[:, vals] for piece in pieces], axis=0)
            mixed = jnp.dot(
                weights, jnp.concatenate((values, ones), axis=1), preferred_element_type=jnp.float32
            )
            out[here, cols] = mixed[:, :HD]
            out[here, WIDTH + head : WIDTH + head + 1] = raised
            out[here, WIDTH + HEADS_HERE + head : WIDTH + HEADS_HERE + head + 1] = mixed[:, HD : HD + 1]


def attend_whole(q, pieces, block=256):
    return pl.pallas_call(
        functools.partial(attend_whole_kernel, block),
        out_shape=jax.ShapeDtypeStruct((q.shape[0], WIDTH + HD), jnp.float32),
        compiler_params=pltpu.CompilerParams(vmem_limit_bytes=20 << 20),
        name="attend_whole",
    )(q, *pieces)


def join_kernel(count, *refs):
    outs = refs[-count:]
    each = (len(refs) - count) // count
    for index, out in enumerate(outs):
        join_one(False, refs[index * each : (index + 1) * each], out)


def join_last_kernel(*refs):
    *parts, out = refs
    join_one(True, parts, out)


def join_one(last, parts, out):
    stats = [part[:, WIDTH:] for part in parts]
    top = functools.reduce(jnp.maximum, stats)
    scales = [jnp.exp2(stat - top) for stat in stats]
    total = sum(pltpu.roll(stat, HD - HEADS_HERE, axis=1) * scale for stat, scale in zip(stats, scales))
    if last:
        inverse = 1.0 / total
        scales = [scale * inverse for scale in scales]
    else:
        out[:, WIDTH:] = jnp.zeros((top.shape[0], HD), jnp.float32)
        out[:, WIDTH : WIDTH + HEADS_HERE] = top[:, :HEADS_HERE]
        out[:, WIDTH + HEADS_HERE : WIDTH + 2 * HEADS_HERE] = total[:, :HEADS_HERE]
    for head in range(HEADS_HERE):
        cols = slice(head * HD, (head + 1) * HD)
        out[:, cols] = sum(
            part[:, cols] * scale[:, head : head + 1] for part, scale in zip(parts, scales)
        ).astype(out.dtype)


def join(*groups):
    first = groups[0][0]
    size = sum(part.size for parts in groups for part in parts)
    return pl.pallas_call(
        functools.partial(join_kernel, len(groups)),
        out_shape=(jax.ShapeDtypeStruct(first.shape, jnp.float32),) * len(groups),
        compiler_params=pltpu.CompilerParams(vmem_limit_bytes=12 << 20),
        cost_estimate=pl.CostEstimate(
            flops=3 * size, bytes_accessed=4 * size, transcendentals=HD * first.shape[0]
        ),
        name="join",
    )(*[part for parts in groups for part in parts])


def join_last(parts):
    return pl.pallas_call(
        join_last_kernel,
        out_shape=jax.ShapeDtypeStruct((parts[0].shape[0], WIDTH), jnp.bfloat16),
        compiler_params=pltpu.CompilerParams(vmem_limit_bytes=12 << 20),
        name="join_last",
    )(*parts)


def hop(block, axis, shift):
    return lax.ppermute(block, axis, ring(2 if axis in ("w", "core") else 4, shift))


def per_device(q_tok, k_tok, v_tok, ref_hidden, ref_wk, ref_wv, key_gain):
    rows = q_tok.shape[0]
    barrier = lax.optimization_barrier
    inputs = [pltpu.with_memory_space_constraint(a, pltpu.HBM) for a in (ref_hidden, ref_wk, ref_wv, k_tok, v_tok)]
    own, *sent, beside = project(*inputs)
    arrived = [hop(block, "tensor", shift) for shift, block in zip((1, 2, 3), sent)]
    back, ahead = hop(beside, "y", 1), hop(beside, "y", 3)

    block = norm(own, *arrived, key_gain.reshape(1, HD))
    block, q_late = barrier((block, q_tok))
    paired, q_peer = barrier((hop(block, "w", 1), hop(q_late, "core", 1)))
    block = jnp.concatenate((block, paired), axis=0)
    pieces = [block] + [hop(block, SMALL, s) for s in (1, 3, 2)]
    pieces[1], back, ahead = barrier((pieces[1], back, ahead))
    block = jnp.concatenate(pieces, axis=0)
    late = [hop(block, BULK, s) for s in (1, 3, 2)]
    half = rows // 2
    opposite = [hop(back[:half], "y", 1), hop(ahead[half:], "y", 3)]

    moves = [(i, 0, rows, i * rows, 0, 2 * WIDTH) for i in range(2)]
    peer_a, own_a = attend((q_peer, q_tok), (beside, back), moves)
    opposite, peer_a, own_a = barrier((opposite, peer_a, own_a))
    size = block.shape[0]
    moves = [(0, 0, rows, 0, 0, 2 * WIDTH), (1, 0, size, 2 * rows, 0, 2 * WIDTH)]
    moves += [(2 + i, 0, half, rows + i * half, 0, 2 * WIDTH) for i in range(2)]
    peer_b, own_b = attend((q_peer, q_tok), [ahead, block] + opposite, moves, chunk=2 * rows + size)
    peer_ab, own_ab = join((peer_a, peer_b), (own_a, own_b))
    late, peer_ab, own_ab = barrier((late, peer_ab, own_ab))
    peer_c = attend_whole(q_peer, late)
    from_peer = hop(*join((peer_ab, peer_c)), "core", 1)
    return join_last((own_ab, attend_whole(q_tok, late), from_peer))


def solution(mesh):
    fine = Mesh(
        mesh.devices.reshape(4, 2, 4, 2, 4),
        ("x", "w", "y", "core", "tensor"),
    )
    placed = (
        P(SEQ, "tensor"),
        P(SEQ, "tensor"),
        P(SEQ, "tensor"),
        P(SEQ, "tensor"),
        P("tensor", None),
        P("tensor", None),
        P(),
    )
    return jax.shard_map(
        per_device, mesh=fine, in_specs=placed, out_specs=P(SEQ, "tensor"), check_vma=False
    )
```

```python
import functools

import jax
import jax.numpy as jnp
from jax import lax
from jax.experimental import pallas as pl
from jax.experimental.pallas import tpu as pltpu
from jax.sharding import Mesh
from jax.sharding import PartitionSpec as P

HD = 128
HEADS_HERE = 3
WIDTH = HEADS_HERE * HD
EPSILON = 1e-06
FACTOR = HD**-0.5 * 1.4426950408889634
SEQ = ("x", "w", "y", "core")
SMALL, BULK = "y", "x"


def ring(count, shift):
    return [(i, (i + shift) % count) for i in range(count)]


def project_kernel(hidden, wk, wv, k_tok, v_tok, own, near, far, next_to, beside, rows, weights, sems):
    me = lax.axis_index("tensor")
    first = pltpu.make_async_copy(hidden, rows, sems.at[8])
    first.start()
    copies = []
    for place, ahead in enumerate((1, 2, 3, 0)):
        peer = lax.rem(me + ahead, 4)
        cols = pl.ds(pl.multiple_of(peer * WIDTH, WIDTH), WIDTH)
        for half, source in enumerate((wk, wv)):
            slot = 2 * place + half
            copy = pltpu.make_async_copy(source.at[:, cols], weights.at[slot], sems.at[slot])
            copy.start()
            copies.append(copy)
    sides = []
    for half, source in enumerate((k_tok, v_tok)):
        copy = pltpu.make_async_copy(source, beside.at[:, pl.ds(half * WIDTH, WIDTH)], sems.at[9 + half])
        copy.start()
        sides.append(copy)
    first.wait()
    for place, out in enumerate((near, far, next_to, own)):
        for half in range(2):
            slot = 2 * place + half
            copies[slot].wait()
            part = jnp.dot(rows[...], weights[slot], preferred_element_type=jnp.float32)
            out[:, half * WIDTH : (half + 1) * WIDTH] = part.astype(out.dtype)
    for copy in sides:
        copy.wait()


def project(hidden, wk, wv, k_tok, v_tok):
    rows, depth = hidden.shape
    sent = jax.ShapeDtypeStruct((rows, 2 * WIDTH), jnp.bfloat16)
    vmem, anywhere = pl.BlockSpec(memory_space=pltpu.VMEM), pl.BlockSpec(memory_space=pl.ANY)
    return pl.pallas_call(
        project_kernel,
        out_shape=(
            jax.ShapeDtypeStruct((rows, 2 * WIDTH), jnp.float32),
            sent,
            sent,
            sent,
            jax.ShapeDtypeStruct((k_tok.shape[0], 2 * WIDTH), jnp.bfloat16),
        ),
        in_specs=[anywhere] * 5,
        out_specs=(vmem,) * 4 + (anywhere,),
        scratch_shapes=[
            pltpu.VMEM((rows, depth), jnp.bfloat16),
            pltpu.VMEM((8, depth, WIDTH), jnp.bfloat16),
            pltpu.SemaphoreType.DMA((11,)),
        ],
        compiler_params=pltpu.CompilerParams(vmem_limit_bytes=8 << 20),
        cost_estimate=pl.CostEstimate(
            flops=2 * rows * depth * 8 * WIDTH, bytes_accessed=2 * depth * 8 * WIDTH, transcendentals=0
        ),
        name="project",
    )(hidden, wk, wv, k_tok, v_tok)


def norm_kernel(own, a, b, c, gain, out):
    total = (
        own[...]
        + a[...].astype(jnp.float32)
        + b[...].astype(jnp.float32)
        + c[...].astype(jnp.float32)
    )
    for head in range(HEADS_HERE):
        cols = slice(head * HD, (head + 1) * HD)
        raw = total[:, cols]
        scale = lax.rsqrt(jnp.mean(raw * raw, axis=1, keepdims=True) + EPSILON)
        out[:, cols] = (raw * scale * gain[...]).astype(jnp.bfloat16)
    out[:, WIDTH:] = total[:, WIDTH:].astype(jnp.bfloat16)


def norm(own, a, b, c, gain):
    rows = own.shape[0]
    return pl.pallas_call(
        norm_kernel,
        out_shape=jax.ShapeDtypeStruct((rows, 2 * WIDTH), jnp.bfloat16),
        compiler_params=pltpu.CompilerParams(vmem_limit_bytes=2 << 20),
        cost_estimate=pl.CostEstimate(flops=10 * own.size, bytes_accessed=12 * own.size, transcendentals=128),
        name="norm",
    )(own, a, b, c, gain)


def attend_whole_kernel(block, count_q, *refs):
    queries, pieces, outs = refs[:count_q], refs[count_q:-count_q], refs[-count_q:]
    keys = sum(piece.shape[0] for piece in pieces)
    ones = jnp.ones((keys, HD), jnp.bfloat16)
    for which, low in [(which, low) for which in range(count_q) for low in range(0, queries[0].shape[0], block)]:
        q, out = queries[which], outs[which]
        here = slice(low, low + block)
        out[here, WIDTH:] = jnp.zeros((block, HD), jnp.float32)
        for head in range(HEADS_HERE):
            cols = slice(head * HD, (head + 1) * HD)
            vals = slice(WIDTH + head * HD, WIDTH + (head + 1) * HD)
            scores = lax.dot_general(
                q[here, cols],
                jnp.concatenate([piece[:, cols] for piece in pieces], axis=0),
                (((1,), (1,)), ((), ())),
                preferred_element_type=jnp.float32,
            )
            raised = jnp.max(scores, axis=1, keepdims=True) * FACTOR
            weights = jnp.exp2(scores * FACTOR - raised).astype(jnp.bfloat16)
            values = jnp.concatenate([piece[:, vals] for piece in pieces], axis=0)
            mixed = jnp.dot(
                weights, jnp.concatenate((values, ones), axis=1), preferred_element_type=jnp.float32
            )
            out[here, cols] = mixed[:, :HD]
            out[here, WIDTH + head : WIDTH + head + 1] = raised
            out[here, WIDTH + HEADS_HERE + head : WIDTH + HEADS_HERE + head + 1] = mixed[:, HD : HD + 1]


def attend_whole(queries, pieces, block=256):
    shape = jax.ShapeDtypeStruct((queries[0].shape[0], WIDTH + HD), jnp.float32)
    return pl.pallas_call(
        functools.partial(attend_whole_kernel, block, len(queries)),
        out_shape=(shape,) * len(queries),
        compiler_params=pltpu.CompilerParams(vmem_limit_bytes=20 << 20),
        name="attend_whole",
    )(*queries, *pieces)


def join_kernel(count, *refs):
    outs = refs[-count:]
    each = (len(refs) - count) // count
    for index, out in enumerate(outs):
        join_one(False, refs[index * each : (index + 1) * each], out)


def join_last_kernel(*refs):
    *parts, out = refs
    join_one(True, parts, out)


def join_one(last, parts, out):
    stats = [part[:, WIDTH:] for part in parts]
    top = functools.reduce(jnp.maximum, stats)
    scales = [jnp.exp2(stat - top) for stat in stats]
    total = sum(pltpu.roll(stat, HD - HEADS_HERE, axis=1) * scale for stat, scale in zip(stats, scales))
    if last:
        inverse = 1.0 / total
        scales = [scale * inverse for scale in scales]
    else:
        out[:, WIDTH:] = jnp.zeros((top.shape[0], HD), jnp.float32)
        out[:, WIDTH : WIDTH + HEADS_HERE] = top[:, :HEADS_HERE]
        out[:, WIDTH + HEADS_HERE : WIDTH + 2 * HEADS_HERE] = total[:, :HEADS_HERE]
    for head in range(HEADS_HERE):
        cols = slice(head * HD, (head + 1) * HD)
        out[:, cols] = sum(
            part[:, cols] * scale[:, head : head + 1] for part, scale in zip(parts, scales)
        ).astype(out.dtype)


def join(*groups):
    first = groups[0][0]
    size = sum(part.size for parts in groups for part in parts)
    return pl.pallas_call(
        functools.partial(join_kernel, len(groups)),
        out_shape=(jax.ShapeDtypeStruct(first.shape, jnp.float32),) * len(groups),
        compiler_params=pltpu.CompilerParams(vmem_limit_bytes=12 << 20),
        cost_estimate=pl.CostEstimate(
            flops=3 * size, bytes_accessed=4 * size, transcendentals=HD * first.shape[0]
        ),
        name="join",
    )(*[part for parts in groups for part in parts])


def join_last(parts):
    return pl.pallas_call(
        join_last_kernel,
        out_shape=jax.ShapeDtypeStruct((parts[0].shape[0], WIDTH), jnp.bfloat16),
        compiler_params=pltpu.CompilerParams(vmem_limit_bytes=12 << 20),
        name="join_last",
    )(*parts)


def hop(block, axis, shift):
    return lax.ppermute(block, axis, ring(2 if axis in ("w", "core") else 4, shift))


def per_device(q_tok, k_tok, v_tok, ref_hidden, ref_wk, ref_wv, key_gain):
    rows = q_tok.shape[0]
    barrier = lax.optimization_barrier
    inputs = [pltpu.with_memory_space_constraint(a, pltpu.HBM) for a in (ref_hidden, ref_wk, ref_wv, k_tok, v_tok)]
    own, *sent, beside = project(*inputs)
    arrived = [hop(block, "tensor", shift) for shift, block in zip((1, 2, 3), sent)]
    back, ahead = hop(beside, "y", 1), hop(beside, "y", 3)

    block = norm(own, *arrived, key_gain.reshape(1, HD))
    block, q_late = barrier((block, q_tok))
    paired, q_peer = barrier((hop(block, "w", 1), hop(q_late, "core", 1)))
    block = jnp.concatenate((block, paired), axis=0)
    pieces = [block] + [hop(block, SMALL, s) for s in (1, 3, 2)]
    pieces[1], back, ahead = barrier((pieces[1], back, ahead))
    block = jnp.concatenate(pieces, axis=0)
    late = [hop(block, BULK, s) for s in (1, 3, 2)]
    half = rows // 2
    opposite = [hop(back[:half], "y", 1), hop(ahead[half:], "y", 3)]

    peer_a, own_a = attend_whole((q_peer, q_tok), (beside, back))
    opposite, peer_a, own_a = barrier((opposite, peer_a, own_a))
    peer_b, own_b = attend_whole((q_peer, q_tok), [ahead, block] + opposite)
    peer_ab, own_ab = join((peer_a, peer_b), (own_a, own_b))
    late, peer_ab, own_ab = barrier((late, peer_ab, own_ab))
    (peer_c,) = attend_whole((q_peer,), late)
    from_peer = hop(*join((peer_ab, peer_c)), "core", 1)
    (own_c,) = attend_whole((q_tok,), late)
    return join_last((own_ab, own_c, from_peer))


def solution(mesh):
    fine = Mesh(
        mesh.devices.reshape(4, 2, 4, 2, 4),
        ("x", "w", "y", "core", "tensor"),
    )
    placed = (
        P(SEQ, "tensor"),
        P(SEQ, "tensor"),
        P(SEQ, "tensor"),
        P(SEQ, "tensor"),
        P("tensor", None),
        P("tensor", None),
        P(),
    )
    return jax.shard_map(
        per_device, mesh=fine, in_specs=placed, out_specs=P(SEQ, "tensor"), check_vma=False
    )
```
